32 devices in a mesh: parts: 2 (over x), ctx: 4 (over z), branch: 4 (over y, core).
Axes of the slice: x: 2, y: 2, z: 4, core: 2. Of those that a mesh axis runs over, the one named last changes fastest.
Arguments:
- prefix_kv: bfloat16 [2, 8192, 1024], P(None, ('parts', 'ctx')), parts along dimension 1
- queries: bfloat16 [512, 8192], P(('parts', 'ctx', 'branch')), parts along dimension 0
- new_kv: bfloat16 [2, 512, 1024], P(None, ('parts', 'ctx', 'branch')), parts along dimension 1, may hold values from -6 to 6
- suffix_kv: bfloat16 [2, 512, 64, 1024], P(None, ('parts', 'ctx', 'branch')), parts along dimension 1, may hold values from -6 to 6
- suffix_len: int32 [512], P(('parts', 'ctx', 'branch')), parts along dimension 0, may hold values from 1 to 64, as said below
- node_kv: bfloat16 [2, 8, 128, 1024], P(None, ('parts', 'branch')), parts along dimension 1, may hold values from -6 to 6
- node_len: int32 [8], P('parts'), parts along dimension 0, may hold values from 1 to 128, as said below
- parent: int32 [8], P('parts'), parts along dimension 0, may hold values from -1 to 2, as said below
- leaf: int32 [512], P(('parts', 'ctx', 'branch')), parts along dimension 0, may hold values from 0 to 3
Outputs:
- context: bfloat16 [512, 8192], P(('parts', 'ctx', 'branch')), parts along dimension 0
The draws below stay inside these ranges and needn't reach their ends.
There are 2 independent parts, one for each index of `parts`. The reference program is written for one: setup_inputs(seed, part) draws one part's arguments, and reference() takes and returns one part's arrays. A program takes and returns all parts, laid end to end along the dimension named above; each array names one. Nothing has to cross between parts.
Inputs may be any that keep to these rules, and one draw needn't show every extreme that they name: `suffix_len`: live tokens stand first in a rollout's suffix; some rollout has all 64. `node_len`: live tokens stand first in a node; some node has all 128. parent[n] is -1 or a node below n; parent[0] is -1.
All inputs are finite; a program needn't handle non-finite values.
Results may differ from the reference program's by a relative error of at most 0.0055.
Values may be sent and summed in bfloat16 or wider, within the bound.
A program may use at most 128 MiB of HBM per device.

```python
import math
import jax
import jax.numpy as jnp
from jax import lax

HEADS = 64
KV_HEADS = 8
HEAD_DIM = 128
R_DEV = 16
NODE_LEN = 128
SUF = 64
QW = 8192
KVW = 1024
PREFIX = 4096
ROLLOUTS = 256
NODES = 4


def draw_prefix_kv(key, part):
    bulk = jax.random.normal(jax.random.fold_in(key, 11), (2, PREFIX, KVW), jnp.float32)
    return bulk.astype(jnp.bfloat16)


def draw_queries(key, part):
    bulk = 2.5 * jax.random.normal(jax.random.fold_in(key, 19), (ROLLOUTS, HEADS, HEAD_DIM), jnp.float32)
    return bulk.reshape(ROLLOUTS, QW).astype(jnp.bfloat16)


def draw_suffix_len(key, part):
    blocks = ROLLOUTS // R_DEV
    caps = jax.random.randint(jax.random.fold_in(key, 31), (blocks, 1), max(SUF // 4, 1), SUF + 1)
    lengths = jax.random.randint(jax.random.fold_in(key, 32), (blocks, R_DEV), 1, caps + 1).reshape(ROLLOUTS)
    spot = jax.random.randint(jax.random.fold_in(key, 33), (), 0, ROLLOUTS)
    return lengths.at[spot].set(SUF).astype(jnp.int32)


def draw_node_len(key, part):
    lengths = jax.random.randint(jax.random.fold_in(key, 41), (NODES,), 1, NODE_LEN + 1)
    spot = jax.random.randint(jax.random.fold_in(key, 42), (), 0, NODES)
    return lengths.at[spot].set(NODE_LEN).astype(jnp.int32)


def draw_parent(key, part):
    upper = jnp.arange(NODES, dtype=jnp.int32)
    drawn = jax.random.randint(jax.random.fold_in(key, 51), (NODES,), -1, upper).astype(jnp.int32)
    drawn = drawn.at[NODES - 1].set(NODES - 2)
    second = (jnp.asarray(part, jnp.int32) % 2 - 1).astype(jnp.int32)
    drawn = drawn.at[1].set(second)
    return drawn.at[0].set(-1).astype(jnp.int32)


def touch_ends(values, key, smallest, largest):
    longest = values.shape.index(max(values.shape))
    spots = []
    for shift in (0, 1):
        where = [jax.random.randint(jax.random.fold_in(key, axis), (), 0, length) for axis, length in enumerate(values.shape)]
        where[longest] = (where[longest] + shift) % values.shape[longest]
        spots.append(tuple(where))
    return values.at[spots[0]].set(smallest).at[spots[1]].set(largest)


def block_scale(key, shape, shards, smallest, top_value):
    loudness, own = 1.0, jax.random.fold_in(key, 6)
    for position, shards_of in shards:
        draws = jnp.exp(jax.random.uniform(jax.random.fold_in(own, position), (shards_of,), jnp.float32, smallest / len(shards), top_value / len(shards)))
        loudness = loudness * jnp.repeat(draws, shape[position] // shards_of).reshape([-1 if axis == position else 1 for axis in range(len(shape))])
    return loudness


def normal_values(stream_key, dims, scale, most, shards=(), kind=jnp.bfloat16):
    entries = scale * jax.random.normal(stream_key, dims, jnp.float32)
    if shards:
        entries = entries * block_scale(stream_key, dims, shards, -0.22, 0.18)
    return jnp.clip(entries, -most, most).astype(kind)


def setup_inputs(seed: int = 0, part: int = 0) -> dict:
    arg_keys = jax.random.split(jax.random.key(seed), 10)
    own_keys = jax.random.split(jax.random.fold_in(arg_keys[9], part), 10)
    prefix_kv = draw_prefix_kv(jax.random.fold_in(jax.random.fold_in(arg_keys[9], part), 71), part)
    queries = draw_queries(jax.random.fold_in(jax.random.fold_in(arg_keys[9], part), 71), part)
    new_kv = normal_values(own_keys[2], (2, ROLLOUTS, KVW), 1.0, 6.0, ((1, 16),))
    suffix_kv = normal_values(own_keys[3], (2, ROLLOUTS, SUF, KVW), 1.0, 6.0, ((1, 16),))
    suffix_len = draw_suffix_len(jax.random.fold_in(jax.random.fold_in(arg_keys[9], part), 71), part)
    node_kv = normal_values(own_keys[5], (2, NODES, NODE_LEN, KVW), 1.0, 6.0, ((1, 4),))
    node_len = draw_node_len(jax.random.fold_in(jax.random.fold_in(arg_keys[9], part), 71), part)
    parent = draw_parent(jax.random.fold_in(jax.random.fold_in(arg_keys[9], part), 71), part)
    leaf = touch_ends(jax.random.randint(own_keys[8], (ROLLOUTS,), 0, NODES), jax.random.fold_in(own_keys[8], 1), 0, NODES - 1).astype(jnp.int32)
    return {"prefix_kv": prefix_kv, "queries": queries, "new_kv": new_kv, "suffix_kv": suffix_kv, "suffix_len": suffix_len, "node_kv": node_kv, "node_len": node_len, "parent": parent, "leaf": leaf}


def reference(prefix_kv, queries, new_kv, suffix_kv, suffix_len, node_kv, node_len, parent, leaf):
    group = HEADS // KV_HEADS
    inverse_root = 1.0 / math.sqrt(HEAD_DIM)
    node_ids = jnp.arange(NODES, dtype=jnp.int32)
    current = node_ids
    ancestry = jnp.zeros((NODES, NODES), dtype=bool)
    for climb_step in range(NODES):
        ancestry = ancestry | (current[:, None] == node_ids[None, :])
        current = jnp.where(current >= 0, parent[jnp.maximum(current, 0)], -1).astype(jnp.int32)
    member = ancestry[leaf]
    node_live = jnp.arange(NODE_LEN, dtype=jnp.int32)[None, :] < node_len[:, None]
    prefix_keys = prefix_kv[0].astype(jnp.float32).reshape(PREFIX, KV_HEADS, HEAD_DIM)
    prefix_values = prefix_kv[1].astype(jnp.float32).reshape(PREFIX, KV_HEADS, HEAD_DIM)
    node_keys = node_kv[0].astype(jnp.float32).reshape(NODES * NODE_LEN, KV_HEADS, HEAD_DIM)
    node_values = node_kv[1].astype(jnp.float32).reshape(NODES * NODE_LEN, KV_HEADS, HEAD_DIM)
    suffix_pos = jnp.arange(SUF, dtype=jnp.int32)
    node_tokens = NODES * NODE_LEN

    def one_block(inputs):
        query_rows, member_rows, suffix_keys, suffix_values, lengths, fresh_keys, fresh_values = inputs
        count = query_rows.shape[0]
        query_heads = query_rows.astype(jnp.float32).reshape(count, KV_HEADS, group, HEAD_DIM)
        prefix_scores = jnp.einsum('bhgd,thd->bhgt', query_heads, prefix_keys) * inverse_root
        node_mask = (member_rows[:, :, None] & node_live[None, :, :]).reshape(count, node_tokens)
        node_scores = jnp.einsum('bhgd,thd->bhgt', query_heads, node_keys) * inverse_root
        node_scores = jnp.where(node_mask[:, None, None, :], node_scores, -jnp.inf)
        suffix_keys_f = suffix_keys.astype(jnp.float32)
        suffix_scores = jnp.einsum('bhgd,bshd->bhgs', query_heads, suffix_keys_f) * inverse_root
        suffix_mask = suffix_pos[None, :] < lengths[:, None]
        suffix_scores = jnp.where(suffix_mask[:, None, None, :], suffix_scores, -jnp.inf)
        fresh_scores = jnp.einsum('bhgd,bhd->bhg', query_heads, fresh_keys.astype(jnp.float32))[..., None] * inverse_root
        scores = jnp.concatenate([prefix_scores, node_scores, suffix_scores, fresh_scores], axis=-1)
        peak = lax.optimization_barrier(jnp.max(scores, axis=-1))
        weights = jnp.exp(scores - peak[..., None])
        totals = lax.optimization_barrier(jnp.sum(weights, axis=-1))
        rounded = lax.optimization_barrier(weights.astype(jnp.bfloat16)).astype(jnp.float32)
        mixed = jnp.einsum('bhgt,thd->bhgd', rounded[..., :PREFIX], prefix_values)
        mixed = mixed + jnp.einsum('bhgt,thd->bhgd', rounded[..., PREFIX:PREFIX + node_tokens], node_values)
        mixed = mixed + jnp.einsum('bhgs,bshd->bhgd', rounded[..., PREFIX + node_tokens:PREFIX + node_tokens + SUF], suffix_values.astype(jnp.float32))
        mixed = mixed + rounded[..., -1:] * fresh_values.astype(jnp.float32)[:, :, None, :]
        return (mixed / totals[..., None]).astype(jnp.bfloat16).reshape(count, QW)
    blocks = ROLLOUTS // R_DEV
    inputs = (queries.reshape(blocks, R_DEV, QW), member.reshape(blocks, R_DEV, NODES), suffix_kv[0].reshape(blocks, R_DEV, SUF, KV_HEADS, HEAD_DIM), suffix_kv[1].reshape(blocks, R_DEV, SUF, KV_HEADS, HEAD_DIM), suffix_len.reshape(blocks, R_DEV), new_kv[0].reshape(blocks, R_DEV, KV_HEADS, HEAD_DIM), new_kv[1].reshape(blocks, R_DEV, KV_HEADS, HEAD_DIM))
    return lax.map(one_block, inputs).reshape(ROLLOUTS, QW)
```

```python
import functools
import math

import jax
import jax.numpy as jnp
from jax import lax
from jax.experimental import pallas as pl
from jax.experimental.pallas import tpu as pltpu
from jax.sharding import PartitionSpec as P

HEADS = 64
KV_HEADS = 8
HEAD_DIM = 128
NODE_LEN = 128
GROUP = HEADS // KV_HEADS
GW = GROUP * HEAD_DIM
MESH = pl.DeviceIdType.MESH
LOG2E = math.log2(math.e)
COEF = HEAD_DIM ** (-0.5) * LOG2E


def dot_t(keys, rows):
    return lax.dot_general(keys, rows, (((1,), (1,)), ((), ())), preferred_element_type=jnp.float32)
EARLY = 5
REST = KV_HEADS - EARLY
HOP = 5
OFFSET = 1
CHUNKS = 4
WIDE = 4
WHOLE_AT = 6
PASS_AT = 6
NODE_AT = 24
NODE_END = 22
FINAL_AT = 27


def kernel(
    n, nb, suffix_len_hbm, node_len_hbm, parent_hbm, leaf_hbm, q_hbm, new_hbm, prefix_hbm, suffix_hbm, node_hbm,
    out_ref,
    suffix_len, node_len, parent, leaf, new_ref, prefix, suffix, nodes, vt, qg,
    o_part, l_part, o_out, l_out, o_in, l_in, o_loc, l_loc, staged,
    load_sem, out_sem, q_send, q_recv, r_send, r_recv, l_send, l_recv, n_send, n_pass, n_recv,
):
    c = lax.axis_index("ctx")
    b = lax.axis_index("branch")
    rollouts = qg.shape[1]
    rows = rollouts * GROUP
    node_count = node_len.shape[0]
    suf = suffix.shape[2]
    chips = nb // 2
    core = lax.rem(b, 2)
    twin = b + 1 - 2 * core
    middle = (c >= 1) & (c + 1 < n)
    wide = KV_HEADS // CHUNKS

    barrier = pltpu.get_barrier_semaphore()
    @pl.when(c + 1 < n)
    def _():
        pl.semaphore_signal(barrier, inc=1, device_id={"ctx": c + 1}, device_id_type=MESH)

    @pl.when(c >= 1)
    def _():
        pl.semaphore_signal(barrier, inc=1, device_id={"ctx": c - 1}, device_id_type=MESH)

    pl.semaphore_signal(barrier, inc=1, device_id={"branch": twin}, device_id_type=MESH)
    for k in range(1, chips):
        pl.semaphore_signal(barrier, inc=1, device_id={"branch": lax.rem(b + 2 * k, nb)}, device_id_type=MESH)

    loads = [
        pltpu.make_async_copy(src, dst, load_sem.at[i])
        for i, (src, dst) in enumerate([
            (q_hbm, qg.at[c]), (prefix_hbm, prefix), (suffix_hbm, suffix), (node_hbm, nodes.at[b]),
            (new_hbm, new_ref), (suffix_len_hbm, suffix_len), (node_len_hbm, node_len),
            (parent_hbm, parent), (leaf_hbm, leaf)])
    ]
    for load in loads:
        load.start()

    @pl.when((c >= 1) & (c + 1 < n))
    def _():
        pl.semaphore_wait(barrier, chips + 2)

    @pl.when((c == 0) | (c == n - 1))
    def _():
        pl.semaphore_wait(barrier, chips + 1)

    def cols(g):
        return pl.ds(pl.multiple_of(g * GW, GW), GW)

    def head_cols(g):
        return pl.ds(pl.multiple_of(g * HEAD_DIM, HEAD_DIM), HEAD_DIM)

    def chunk_cols(j):
        return pl.ds(pl.multiple_of(j * wide * HEAD_DIM, wide * HEAD_DIM), wide * HEAD_DIM)

    def own_copy(side, target, g):
        return pltpu.make_async_remote_copy(
            src_ref=q_hbm.at[:, cols(g)], dst_ref=qg.at[c, :, cols(g)],
            send_sem=q_send.at[side, c, g], recv_sem=q_recv.at[c, g],
            device_id={"ctx": target}, device_id_type=MESH)

    def pass_copy(side, src, target, g):
        return pltpu.make_async_remote_copy(
            src_ref=qg.at[src, :, cols(g)], dst_ref=qg.at[src, :, cols(g)],
            send_sem=q_send.at[side, src, g], recv_sem=q_recv.at[src, g],
            device_id={"ctx": target}, device_id_type=MESH)

    def result_copies(dest, side, target, g):
        return (
            pltpu.make_async_remote_copy(
                src_ref=o_out.at[dest, g], dst_ref=o_in.at[side, dest, g],
                send_sem=r_send.at[dest, g], recv_sem=r_recv.at[side, dest, g],
                device_id={"ctx": target}, device_id_type=MESH),
            pltpu.make_async_remote_copy(
                src_ref=l_out.at[dest, g], dst_ref=l_in.at[side, dest, g],
                send_sem=l_send.at[dest, g], recv_sem=l_recv.at[side, dest, g],
                device_id={"ctx": target}, device_id_type=MESH))

    def node_copy(peer, slot, sem, j):
        return pltpu.make_async_remote_copy(
            src_ref=node_hbm.at[:, :, :, chunk_cols(j)], dst_ref=nodes.at[slot, :, :, :, chunk_cols(j)],
            send_sem=sem.at[j], recv_sem=n_recv.at[slot, j], device_id={"branch": peer}, device_id_type=MESH)

    def node_pass(slot, sem, j):
        return pltpu.make_async_remote_copy(
            src_ref=nodes.at[slot, :, :, :, chunk_cols(j)], dst_ref=nodes.at[slot, :, :, :, chunk_cols(j)],
            send_sem=sem.at[j], recv_sem=n_recv.at[slot, j], device_id={"branch": twin}, device_id_type=MESH)

    @pl.loop(0, KV_HEADS)
    def _(g):
        @pl.when((c + 1 < n) & ((c == 0) | (g < EARLY)))
        def _():
            own_copy(0, c + 1, g).start()

        @pl.when((c >= 1) & ((c == n - 1) | (g < EARLY)))
        def _():
            own_copy(1, c - 1, g).start()

    for j in range(CHUNKS):
        for k in range(1, chips):
            node_copy(lax.rem(b + 2 * k, nb), b, n_send.at[k], j).start()
    for j in range(CHUNKS):
        node_copy(twin, b, n_send.at[0], j).start()

    for load in loads[5:]:
        load.wait()
    lane = lax.rem(lax.broadcasted_iota(jnp.int32, (1, rows), 1), rollouts)
    lengths = jnp.zeros((1, rows), jnp.int32)
    current = jnp.zeros((1, rows), jnp.int32)
    for r in range(rollouts):
        lengths = jnp.where(lane == r, suffix_len[r], lengths)
        current = jnp.where(lane == r, leaf[r], current)
    limits = [jnp.zeros((1, rows), jnp.int32) for _ in range(node_count)]
    for _ in range(node_count):
        lifted = jnp.full((1, rows), -1, jnp.int32)
        for node in range(node_count):
            hit = current == node
            limits[node] = jnp.where(hit, node_len[node], limits[node])
            lifted = jnp.where(hit, parent[node], lifted)
        current = lifted
    chosen = [(lane == r) for r in range(rollouts)]
    picked = [hit.astype(jnp.bfloat16) for hit in chosen]

    for side, alone in ((0, c == n - 1), (1, c == 0)):
        @pl.when(alone)
        def _():
            @pl.loop(0, KV_HEADS)
            def _(g):
                o_in[side, c, g] = jnp.zeros((HEAD_DIM, rows), jnp.bfloat16)
                l_in[side, c, g] = jnp.full((1, rows), -jnp.inf, jnp.float32)

    def stack(block):
        return [block[:, j * HEAD_DIM:(j + 1) * HEAD_DIM] for j in range(GROUP)]

    def arrival(u, sources):
        block = EARLY * (sources - 1)
        v, w = u - block, u - block - KV_HEADS
        early, late = u < block, v >= KV_HEADS
        distance = jnp.where(early, u // EARLY + 1, jnp.where(late, sources - 1 - w // REST, sources))
        g = jnp.where(early, u % EARLY, jnp.where(late, EARLY + w % REST, v))
        return distance, g

    def relay(u):
        distance, g = arrival(u, c)

        @pl.when((u >= 0) & (u < KV_HEADS * c))
        def _():
            src = c - distance
            pass_copy(0, src, src, g).wait_recv()

            @pl.when(c + 1 < n)
            def _():
                pass_copy(0, src, c + 1, g).start()

                @pl.when(u == KV_HEADS * c - 1)
                def _():
                    for h in range(EARLY, KV_HEADS):
                        own_copy(0, c + 1, h).start()

        back, h = arrival(u, n - 1 - c)

        @pl.when((u >= 0) & (u < KV_HEADS * (n - 1 - c)))
        def _():
            src = c + back
            pass_copy(1, src, src, h).wait_recv()

            @pl.when(c >= 1)
            def _():
                pass_copy(1, src, c - 1, h).start()

                @pl.when(u == KV_HEADS * (n - 1 - c) - 1)
                def _():
                    for k in range(EARLY, KV_HEADS):
                        own_copy(1, c - 1, k).start()

    def launch(dest, side, g):
        for copy in result_copies(dest, side, c - 1 if side == 0 else c + 1, g):
            copy.start()

    def attend(keys, values, query):
        scores = dot_t(keys, query)
        peak = jnp.max(scores, axis=0, keepdims=True) * COEF
        weights = jnp.exp2(scores * COEF - peak)
        total = jnp.sum(weights, axis=0, keepdims=True)
        mixed = jnp.dot(values, weights.astype(jnp.bfloat16), preferred_element_type=jnp.float32)
        return mixed * (1.0 / total), peak + jnp.log2(total)

    def pair_item(src, g):
        query = jnp.concatenate(stack(qg[c, :, cols(g)]) + stack(qg[src, :, cols(g)]), axis=0)
        mixed, stat = attend(prefix[0, :, head_cols(g)], vt[g], query)
        o_part[c, g] = mixed[:, :rows]
        l_part[c, g] = stat[:, :rows]
        o_out[src, g] = mixed[:, rows:].astype(jnp.bfloat16)
        l_out[src, g] = stat[:, rows:]

    def single_item(src, g):
        query = jnp.concatenate(stack(qg[src, :, cols(g)]), axis=0)
        mixed, stat = attend(prefix[0, :, head_cols(g)], vt[g], query)
        o_out[src, g] = mixed.astype(jnp.bfloat16)
        l_out[src, g] = stat

    def whole_item(g):
        for base in range(0, n, WIDE):
            dests = range(base, min(base + WIDE, n))
            query = jnp.concatenate([piece for d in dests for piece in stack(qg[d, :, cols(g)])], axis=0)
            mixed, stat = attend(prefix[0, :, head_cols(g)], vt[g], query)
            for k, d in enumerate(dests):
                o_part[d, g] = mixed[:, k * rows:(k + 1) * rows]
                l_part[d, g] = stat[:, k * rows:(k + 1) * rows]

    def emit(src, g):
        @pl.when(c == n - 1)
        def _():
            launch(src, 0, g)

        @pl.when(c == 0)
        def _():
            launch(src, 1, g)

    def merge(dest, side, g):
        for copy in result_copies(dest, side, dest, g):
            copy.wait_recv()
        stat_a, stat_b = l_part[dest, g], l_in[side, dest, g]
        peak = jnp.maximum(stat_a, stat_b)
        share_a, share_b = jnp.exp2(stat_a - peak), jnp.exp2(stat_b - peak)
        total = share_a + share_b
        scale = 1.0 / total
        mixed = o_part[dest, g] * (share_a * scale) + o_in[side, dest, g].astype(jnp.float32) * (share_b * scale)
        o_out[dest, g] = mixed.astype(jnp.bfloat16)
        l_out[dest, g] = peak + jnp.log2(total)
        launch(dest, side, g)

    def suffix_item(g):
        query = jnp.concatenate(stack(qg[c, :, cols(g)]), axis=0)
        keys = suffix[0, :, :, head_cols(g)].reshape(rollouts * suf, HEAD_DIM)
        dense = dot_t(keys, query)
        own = dense[:suf]
        for r in range(1, rollouts):
            own = jnp.where(chosen[r], dense[r * suf:(r + 1) * suf], own)
        spot = lax.broadcasted_iota(jnp.int32, (suf, rows), 0)
        scores = jnp.where(spot < lengths, own, -jnp.inf)
        peak = jnp.max(scores, axis=0, keepdims=True) * COEF
        weights = jnp.exp2(scores * COEF - peak)
        total = jnp.sum(weights, axis=0, keepdims=True)
        weights = weights.astype(jnp.bfloat16)
        spread = jnp.concatenate([weights * picked[r] for r in range(rollouts)], axis=0)
        values = suffix[1, :, :, head_cols(g)].reshape(rollouts * suf, HEAD_DIM)
        mixed = lax.dot_general(values, spread, (((0,), (0,)), ((), ())), preferred_element_type=jnp.float32)
        o_loc[0, g] = mixed / total
        l_loc[0, g] = peak + jnp.log2(total)

    def node_item(g):
        query = jnp.concatenate(stack(qg[c, :, cols(g)]), axis=0)
        pieces, values = [], []
        spot = lax.broadcasted_iota(jnp.int32, (NODE_LEN, rows), 0)
        for node in range(node_count):
            owner, inner = node // nodes.shape[2], node % nodes.shape[2]
            scores = dot_t(nodes[owner, 0, inner, :, head_cols(g)], query)
            pieces.append(jnp.where(spot < limits[node], scores, -jnp.inf))
            values.append(nodes[owner, 1, inner, :, head_cols(g)])
        spot = lax.broadcasted_iota(jnp.int32, (rollouts, rows), 0)
        pieces.append(jnp.where(spot == lane, dot_t(new_ref[0, :, head_cols(g)], query), -jnp.inf))
        values.append(new_ref[1, :, head_cols(g)])
        peak = functools.reduce(jnp.maximum, [jnp.max(s, axis=0, keepdims=True) for s in pieces]) * COEF
        weights = [jnp.exp2(scores * COEF - peak) for scores in pieces]
        total = functools.reduce(jnp.add, [jnp.sum(w, axis=0, keepdims=True) for w in weights])
        mixed = functools.reduce(jnp.add, [
            lax.dot_general(
                block, w.astype(jnp.bfloat16), (((0,), (0,)), ((), ())), preferred_element_type=jnp.float32)
            for block, w in zip(values, weights)])
        o_loc[1, g] = mixed / total
        l_loc[1, g] = peak + jnp.log2(total)

    def out_copy(g):
        return pltpu.make_async_copy(staged.at[:, cols(g)], out_ref.at[:, cols(g)], out_sem.at[g])

    def final(g):
        @pl.when(c + 1 < n)
        def _():
            own_copy(0, c + 1, g).wait_send()
            for copy in result_copies(c, 0, c, g):
                copy.wait_recv()

        @pl.when(c >= 1)
        def _():
            own_copy(1, c - 1, g).wait_send()
            for copy in result_copies(c, 1, c, g):
                copy.wait_recv()

        stats = [l_part[c, g], l_loc[0, g], l_loc[1, g], l_in[0, c, g], l_in[1, c, g]]
        parts = [o_part[c, g], o_loc[0, g], o_loc[1, g], o_in[0, c, g], o_in[1, c, g]]
        peak = functools.reduce(jnp.maximum, stats)
        shares = [jnp.exp2(stat - peak) for stat in stats]
        scale = 1.0 / functools.reduce(jnp.add, shares)
        mixed = functools.reduce(
            jnp.add, [part.astype(jnp.float32) * (share * scale) for part, share in zip(parts, shares)])
        done = mixed.T.astype(jnp.bfloat16)
        for j in range(GROUP):
            staged[:, pl.ds(pl.multiple_of(g * GW + j * HEAD_DIM, HEAD_DIM), HEAD_DIM)] = (
                done[j * rollouts:(j + 1) * rollouts])
        out_copy(g).start()

    loads[0].wait()
    loads[1].wait()
    inner = (c >= 1) & (c + 1 < n)
    outer = jnp.logical_not(inner)
    turn = jnp.where(c == 0, 1, -1)
    arrivals = KV_HEADS * (n - 1)
    ready = WHOLE_AT if n == 4 else KV_HEADS * (n - 2)
    offset = OFFSET if n == 4 else ready + 2 * KV_HEADS
    finals = offset + (FINAL_AT if n == 4 else arrivals + HOP * (n - 1))
    length = max(finals + KV_HEADS, arrivals + HOP * (n - 2) + offset, ready + 2 * KV_HEADS, PASS_AT + 16, NODE_AT + KV_HEADS)
    for load in loads[2:5]:
        load.wait()

    @pl.loop(0, KV_HEADS // 2)
    def _(s):
        for k in range(2):
            vt[2 * s + k] = prefix[1, :, head_cols(2 * s + k)].T
            suffix_item(2 * s + k)

    @pl.loop(0, length)
    def _(u):
        relay(u)
        distance, g = arrival(u, n - 1)
        src = jnp.clip(c + turn * distance, 0, n - 1)
        busy = outer & (u < arrivals)

        @pl.when(busy & (distance == 1))
        def _():
            pair_item(src, g)

        @pl.when(busy & (distance > 1))
        def _():
            single_item(src, g)

        @pl.when(busy)
        def _():
            emit(src, g)

        for j in range(CHUNKS):
            @pl.when(u == PASS_AT + 4 * j)
            def _():
                for k in range(1, chips):
                    peer = lax.rem(b + 2 * k, nb)
                    node_pass(peer, n_pass.at[k], j).wait_recv()
                    node_pass(peer, n_pass.at[k], j).start()

        whole = u - ready

        @pl.when(inner & (whole >= 0) & (whole < 2 * KV_HEADS) & (whole % 2 == 0))
        def _():
            whole_item(whole // 2)

        for side, hops in ((0, n - 1 - c), (1, c)):
            x = u - offset - HOP * hops
            far, h = arrival(x, n - 1)
            dest = n - 1 - far if side == 0 else far
            onward = (dest < c) if side == 0 else (dest > c)

            @pl.when(inner & (x >= 0) & (x < arrivals) & onward)
            def _():
                merge(dest, side, h)

        w = u - jnp.where(inner, NODE_AT, NODE_END)

        @pl.when((w >= 0) & (w < KV_HEADS) & (w % 2 == 0))
        def _():
            for k in range(chips):
                peer = lax.rem(twin + 2 * k, nb)
                node_pass(peer, n_pass.at[k], w // wide).wait_recv()
            node_item(w)
            node_item(w + 1)

        f = u - finals

        @pl.when((f >= 0) & (f < KV_HEADS))
        def _():
            final(f)

    @pl.loop(0, KV_HEADS)
    def _(g):
        for d in range(1, n):
            @pl.when((c - d >= 0) & (c + 1 < n))
            def _():
                pass_copy(0, c - d, c + 1, g).wait_send()

            @pl.when((c + d < n) & (c >= 1))
            def _():
                pass_copy(1, c + d, c - 1, g).wait_send()

            for copy in result_copies(lax.rem(c + d, n), 0, lax.rem(c + d, n), g):
                copy.wait_send()
        out_copy(g).wait()

    for j in range(CHUNKS):
        for k in range(1, chips):
            node_copy(lax.rem(b + 2 * k, nb), b, n_send.at[k], j).wait_send()
            node_pass(lax.rem(b + 2 * k, nb), n_pass.at[k], j).wait_send()
        node_copy(twin, b, n_send.at[0], j).wait_send()


def on_device(n, nb, prefix_kv, queries, new_kv, suffix_kv, suffix_len, node_kv, node_len, parent, leaf):
    rows = queries.shape[0] * GROUP
    dma = pltpu.SemaphoreType.DMA
    bf16, f32 = jnp.bfloat16, jnp.float32
    return pl.pallas_call(
        functools.partial(kernel, n, nb),
        out_shape=jax.ShapeDtypeStruct(queries.shape, bf16),
        in_specs=[pl.BlockSpec(memory_space=pltpu.HBM)] * 9,
        out_specs=pl.BlockSpec(memory_space=pltpu.HBM),
        scratch_shapes=[
            pltpu.SMEM(suffix_len.shape, jnp.int32),
            pltpu.SMEM(node_len.shape, jnp.int32),
            pltpu.SMEM(parent.shape, jnp.int32),
            pltpu.SMEM(leaf.shape, jnp.int32),
            pltpu.VMEM(new_kv.shape, bf16),
            pltpu.VMEM(prefix_kv.shape, bf16),
            pltpu.VMEM(suffix_kv.shape, bf16),
            pltpu.VMEM((nb,) + node_kv.shape, bf16),
            pltpu.VMEM((KV_HEADS, HEAD_DIM, prefix_kv.shape[1]), bf16),
            pltpu.VMEM((n,) + queries.shape, bf16),
            pltpu.VMEM((n, KV_HEADS, HEAD_DIM, rows), f32),
            pltpu.VMEM((n, KV_HEADS, 1, rows), f32),
            pltpu.VMEM((n, KV_HEADS, HEAD_DIM, rows), bf16),
            pltpu.VMEM((n, KV_HEADS, 1, rows), f32),
            pltpu.VMEM((2, n, KV_HEADS, HEAD_DIM, rows), bf16),
            pltpu.VMEM((2, n, KV_HEADS, 1, rows), f32),
            pltpu.VMEM((2, KV_HEADS, HEAD_DIM, rows), f32),
            pltpu.VMEM((2, KV_HEADS, 1, rows), f32),
            pltpu.VMEM(queries.shape, bf16),
            dma((9,)),
            dma((KV_HEADS,)),
            dma((2, n, KV_HEADS)),
            dma((n, KV_HEADS)),
            dma((n, KV_HEADS)),
            dma((2, n, KV_HEADS)),
            dma((n, KV_HEADS)),
            dma((2, n, KV_HEADS)),
            dma((nb // 2, CHUNKS)),
            dma((nb // 2, CHUNKS)),
            dma((nb, CHUNKS)),
        ],
        compiler_params=pltpu.CompilerParams(
            collective_id=0, has_side_effects=True, vmem_limit_bytes=63 * 1024 * 1024),
    )(suffix_len, node_len, parent, leaf, queries, new_kv, prefix_kv, suffix_kv, node_kv)


def solution(mesh):
    return jax.shard_map(
        functools.partial(on_device, mesh.shape["ctx"], mesh.shape["branch"]),
        mesh=mesh,
        in_specs=(
            P(None, ("parts", "ctx"), None),
            P(("parts", "ctx", "branch"), None),
            P(None, ("parts", "ctx", "branch"), None),
            P(None, ("parts", "ctx", "branch"), None, None),
            P(("parts", "ctx", "branch")),
            P(None, ("parts", "branch"), None, None),
            P("parts"),
            P("parts"),
            P(("parts", "ctx", "branch")),
        ),
        out_specs=P(("parts", "ctx", "branch"), None),
        check_vma=False,
    )
```

```python
import functools
import math

import jax
import jax.numpy as jnp
from jax import lax
from jax.experimental import pallas as pl
from jax.experimental.pallas import tpu as pltpu
from jax.sharding import PartitionSpec as P

HEADS = 64
KV_HEADS = 8
HEAD_DIM = 128
NODE_LEN = 128
GROUP = HEADS // KV_HEADS
GW = GROUP * HEAD_DIM
MESH = pl.DeviceIdType.MESH
LOG2E = math.log2(math.e)
COEF = HEAD_DIM ** (-0.5) * LOG2E


def dot_t(keys, rows):
    return lax.dot_general(keys, rows, (((1,), (1,)), ((), ())), preferred_element_type=jnp.float32)
EARLY = 5
REST = KV_HEADS - EARLY
HOP = 5
OFFSET = 1
CHUNKS = 4
WIDE = 4
WHOLE_AT = 6
PASS_AT = 6
NODE_AT = 24
NODE_END = 22
FINAL_AT = 27


def kernel(
    n, nb, suffix_len_hbm, node_len_hbm, parent_hbm, leaf_hbm, q_hbm, new_hbm, prefix_hbm, suffix_hbm, node_hbm,
    out_ref,
    suffix_len, node_len, parent, leaf, new_ref, prefix, suffix, nodes, vt, qg,
    o_part, l_part, o_out, l_out, o_in, l_in, o_loc, l_loc, staged,
    load_sem, out_sem, q_send, q_recv, r_send, r_recv, l_send, l_recv, n_send, n_pass, n_recv,
):
    c = lax.axis_index("ctx")
    b = lax.axis_index("branch")
    rollouts = qg.shape[1]
    rows = rollouts * GROUP
    node_count = node_len.shape[0]
    suf = suffix.shape[2]
    chips = nb // 2
    core = lax.rem(b, 2)
    twin = b + 1 - 2 * core
    middle = (c >= 1) & (c + 1 < n)
    wide = KV_HEADS // CHUNKS

    barrier = pltpu.get_barrier_semaphore()
    @pl.when(c + 1 < n)
    def _():
        pl.semaphore_signal(barrier, inc=1, device_id={"ctx": c + 1}, device_id_type=MESH)

    @pl.when(c >= 1)
    def _():
        pl.semaphore_signal(barrier, inc=1, device_id={"ctx": c - 1}, device_id_type=MESH)

    pl.semaphore_signal(barrier, inc=1, device_id={"branch": twin}, device_id_type=MESH)
    for k in range(1, chips):
        pl.semaphore_signal(barrier, inc=1, device_id={"branch": lax.rem(b + 2 * k, nb)}, device_id_type=MESH)

    loads = [
        pltpu.make_async_copy(src, dst, load_sem.at[i])
        for i, (src, dst) in enumerate([
            (q_hbm, qg.at[c]), (prefix_hbm, prefix), (suffix_hbm, suffix), (node_hbm, nodes.at[b]),
            (new_hbm, new_ref), (suffix_len_hbm, suffix_len), (node_len_hbm, node_len),
            (parent_hbm, parent), (leaf_hbm, leaf)])
    ]
    for load in loads:
        load.start()

    @pl.when((c >= 1) & (c + 1 < n))
    def _():
        pl.semaphore_wait(barrier, chips + 2)

    @pl.when((c == 0) | (c == n - 1))
    def _():
        pl.semaphore_wait(barrier, chips + 1)

    def cols(g):
        return pl.ds(pl.multiple_of(g * GW, GW), GW)

    def head_cols(g):
        return pl.ds(pl.multiple_of(g * HEAD_DIM, HEAD_DIM), HEAD_DIM)

    def chunk_cols(j):
        return pl.ds(pl.multiple_of(j * wide * HEAD_DIM, wide * HEAD_DIM), wide * HEAD_DIM)

    def own_copy(side, target, g):
        return pltpu.make_async_remote_copy(
            src_ref=q_hbm.at[:, cols(g)], dst_ref=qg.at[c, :, cols(g)],
            send_sem=q_send.at[side, c, g], recv_sem=q_recv.at[c, g],
            device_id={"ctx": target}, device_id_type=MESH)

    def pass_copy(side, src, target, g):
        return pltpu.make_async_remote_copy(
            src_ref=qg.at[src, :, cols(g)], dst_ref=qg.at[src, :, cols(g)],
            send_sem=q_send.at[side, src, g], recv_sem=q_recv.at[src, g],
            device_id={"ctx": target}, device_id_type=MESH)

    def result_copies(dest, side, target, g):
        return (
            pltpu.make_async_remote_copy(
                src_ref=o_out.at[dest, g], dst_ref=o_in.at[side, dest, g],
                send_sem=r_send.at[dest, g], recv_sem=r_recv.at[side, dest, g],
                device_id={"ctx": target}, device_id_type=MESH),
            pltpu.make_async_remote_copy(
                src_ref=l_out.at[dest, g], dst_ref=l_in.at[side, dest, g],
                send_sem=l_send.at[dest, g], recv_sem=l_recv.at[side, dest, g],
                device_id={"ctx": target}, device_id_type=MESH))

    def node_copy(peer, slot, sem, j):
        return pltpu.make_async_remote_copy(
            src_ref=node_hbm.at[:, :, :, chunk_cols(j)], dst_ref=nodes.at[slot, :, :, :, chunk_cols(j)],
            send_sem=sem.at[j], recv_sem=n_recv.at[slot, j], device_id={"branch": peer}, device_id_type=MESH)

    def node_pass(slot, sem, j):
        return pltpu.make_async_remote_copy(
            src_ref=nodes.at[slot, :, :, :, chunk_cols(j)], dst_ref=nodes.at[slot, :, :, :, chunk_cols(j)],
            send_sem=sem.at[j], recv_sem=n_recv.at[slot, j], device_id={"branch": twin}, device_id_type=MESH)

    @pl.loop(0, KV_HEADS)
    def _(g):
        @pl.when((c + 1 < n) & ((c == 0) | (g < EARLY)))
        def _():
            own_copy(0, c + 1, g).start()

        @pl.when((c >= 1) & ((c == n - 1) | (g < EARLY)))
        def _():
            own_copy(1, c - 1, g).start()

    for j in range(CHUNKS):
        for k in range(1, chips):
            node_copy(lax.rem(b + 2 * k, nb), b, n_send.at[k], j).start()
    for j in range(CHUNKS):
        node_copy(twin, b, n_send.at[0], j).start()

    for load in loads[5:]:
        load.wait()
    lane = lax.rem(lax.broadcasted_iota(jnp.int32, (1, rows), 1), rollouts)
    lengths = jnp.zeros((1, rows), jnp.int32)
    current = jnp.zeros((1, rows), jnp.int32)
    for r in range(rollouts):
        lengths = jnp.where(lane == r, suffix_len[r], lengths)
        current = jnp.where(lane == r, leaf[r], current)
    limits = [jnp.zeros((1, rows), jnp.int32) for _ in range(node_count)]
    for _ in range(node_count):
        lifted = jnp.full((1, rows), -1, jnp.int32)
        for node in range(node_count):
            hit = current == node
            limits[node] = jnp.where(hit, node_len[node], limits[node])
            lifted = jnp.where(hit, parent[node], lifted)
        current = lifted
    chosen = [(lane == r) for r in range(rollouts)]
    picked = [hit.astype(jnp.bfloat16) for hit in chosen]

    for side, alone in ((0, c == n - 1), (1, c == 0)):
        @pl.when(alone)
        def _():
            @pl.loop(0, KV_HEADS)
            def _(g):
                o_in[side, c, g] = jnp.zeros((HEAD_DIM, rows), jnp.bfloat16)
                l_in[side, c, g] = jnp.full((1, rows), -jnp.inf, jnp.float32)

    def stack(block):
        return [block[:, j * HEAD_DIM:(j + 1) * HEAD_DIM] for j in range(GROUP)]

    def arrival(u, sources):
        block = EARLY * (sources - 1)
        v, w = u - block, u - block - KV_HEADS
        early, late = u < block, v >= KV_HEADS
        distance = jnp.where(early, u // EARLY + 1, jnp.where(late, sources - 1 - w // REST, sources))
        g = jnp.where(early, u % EARLY, jnp.where(late, EARLY + w % REST, v))
        return distance, g

    def relay(u):
        distance, g = arrival(u, c)

        @pl.when((u >= 0) & (u < KV_HEADS * c))
        def _():
            src = c - distance
            pass_copy(0, src, src, g).wait_recv()

            @pl.when(c + 1 < n)
            def _():
                pass_copy(0, src, c + 1, g).start()

                @pl.when(u == KV_HEADS * c - 1)
                def _():
                    for h in range(EARLY, KV_HEADS):
                        own_copy(0, c + 1, h).start()

        back, h = arrival(u, n - 1 - c)

        @pl.when((u >= 0) & (u < KV_HEADS * (n - 1 - c)))
        def _():
            src = c + back
            pass_copy(1, src, src, h).wait_recv()

            @pl.when(c >= 1)
            def _():
                pass_copy(1, src, c - 1, h).start()

                @pl.when(u == KV_HEADS * (n - 1 - c) - 1)
                def _():
                    for k in range(EARLY, KV_HEADS):
                        own_copy(1, c - 1, k).start()

    def launch(dest, side, g):
        for copy in result_copies(dest, side, c - 1 if side == 0 else c + 1, g):
            copy.start()

    def attend(keys, values, query):
        scores = dot_t(keys, query)
        peak = jnp.max(scores, axis=0, keepdims=True) * COEF
        weights = jnp.exp2(scores * COEF - peak)
        total = jnp.sum(weights, axis=0, keepdims=True)
        mixed = jnp.dot(values, weights.astype(jnp.bfloat16), preferred_element_type=jnp.float32)
        return mixed * (1.0 / total), peak + jnp.log2(total)

    def pair_item(src, g):
        query = jnp.concatenate(stack(qg[c, :, cols(g)]) + stack(qg[src, :, cols(g)]), axis=0)
        mixed, stat = attend(prefix[0, :, head_cols(g)], vt[g], query)
        o_part[c, g] = mixed[:, :rows]
        l_part[c, g] = stat[:, :rows]
        o_out[src, g] = mixed[:, rows:].astype(jnp.bfloat16)
        l_out[src, g] = stat[:, rows:]

    def single_item(src, g):
        query = jnp.concatenate(stack(qg[src, :, cols(g)]), axis=0)
        mixed, stat = attend(prefix[0, :, head_cols(g)], vt[g], query)
        o_out[src, g] = mixed.astype(jnp.bfloat16)
        l_out[src, g] = stat

    def whole_item(g):
        for base in range(0, n, WIDE):
            dests = range(base, min(base + WIDE, n))
            query = jnp.concatenate([piece for d in dests for piece in stack(qg[d, :, cols(g)])], axis=0)
            mixed, stat = attend(prefix[0, :, head_cols(g)], vt[g], query)
            for k, d in enumerate(dests):
                o_part[d, g] = mixed[:, k * rows:(k + 1) * rows]
                l_part[d, g] = stat[:, k * rows:(k + 1) * rows]

    def emit(src, g):
        @pl.when(c == n - 1)
        def _():
            launch(src, 0, g)

        @pl.when(c == 0)
        def _():
            launch(src, 1, g)

    def merge(dest, side, g):
        for copy in result_copies(dest, side, dest, g):
            copy.wait_recv()
        stat_a, stat_b = l_part[dest, g], l_in[side, dest, g]
        peak = jnp.maximum(stat_a, stat_b)
        share_a, share_b = jnp.exp2(stat_a - peak), jnp.exp2(stat_b - peak)
        total = share_a + share_b
        scale = 1.0 / total
        mixed = o_part[dest, g] * (share_a * scale) + o_in[side, dest, g].astype(jnp.float32) * (share_b * scale)
        o_out[dest, g] = mixed.astype(jnp.bfloat16)
        l_out[dest, g] = peak + jnp.log2(total)
        launch(dest, side, g)

    def suffix_item(g):
        query = jnp.concatenate(stack(qg[c, :, cols(g)]), axis=0)
        keys = suffix[0, :, :, head_cols(g)].reshape(rollouts * suf, HEAD_DIM)
        dense = dot_t(keys, query)
        own = dense[:suf]
        for r in range(1, rollouts):
            own = jnp.where(chosen[r], dense[r * suf:(r + 1) * suf], own)
        spot = lax.broadcasted_iota(jnp.int32, (suf, rows), 0)
        scores = jnp.where(spot < lengths, own, -jnp.inf)
        peak = jnp.max(scores, axis=0, keepdims=True) * COEF
        weights = jnp.exp2(scores * COEF - peak)
        total = jnp.sum(weights, axis=0, keepdims=True)
        weights = weights.astype(jnp.bfloat16)
        spread = jnp.concatenate([weights * picked[r] for r in range(rollouts)], axis=0)
        values = suffix[1, :, :, head_cols(g)].reshape(rollouts * suf, HEAD_DIM)
        mixed = lax.dot_general(values, spread, (((0,), (0,)), ((), ())), preferred_element_type=jnp.float32)
        o_loc[0, g] = mixed / total
        l_loc[0, g] = peak + jnp.log2(total)

    def node_item(g):
        query = jnp.concatenate(stack(qg[c, :, cols(g)]), axis=0)
        pieces, values = [], []
        spot = lax.broadcasted_iota(jnp.int32, (NODE_LEN, rows), 0)
        for node in range(node_count):
            owner, inner = node // nodes.shape[2], node % nodes.shape[2]
            scores = dot_t(nodes[owner, 0, inner, :, head_cols(g)], query)
            pieces.append(jnp.where(spot < limits[node], scores, -jnp.inf))
            values.append(nodes[owner, 1, inner, :, head_cols(g)])
        spot = lax.broadcasted_iota(jnp.int32, (rollouts, rows), 0)
        pieces.append(jnp.where(spot == lane, dot_t(new_ref[0, :, head_cols(g)], query), -jnp.inf))
        values.append(new_ref[1, :, head_cols(g)])
        peak = functools.reduce(jnp.maximum, [jnp.max(s, axis=0, keepdims=True) for s in pieces]) * COEF
        weights = [jnp.exp2(scores * COEF - peak) for scores in pieces]
        total = functools.reduce(jnp.add, [jnp.sum(w, axis=0, keepdims=True) for w in weights])
        mixed = functools.reduce(jnp.add, [
            lax.dot_general(
                block, w.astype(jnp.bfloat16), (((0,), (0,)), ((), ())), preferred_element_type=jnp.float32)
            for block, w in zip(values, weights)])
        o_loc[1, g] = mixed / total
        l_loc[1, g] = peak + jnp.log2(total)

    def out_copy(g):
        return pltpu.make_async_copy(staged.at[:, cols(g)], out_ref.at[:, cols(g)], out_sem.at[g])

    def final(g):
        @pl.when(c + 1 < n)
        def _():
            own_copy(0, c + 1, g).wait_send()
            for copy in result_copies(c, 0, c, g):
                copy.wait_recv()

        @pl.when(c >= 1)
        def _():
            own_copy(1, c - 1, g).wait_send()
            for copy in result_copies(c, 1, c, g):
                copy.wait_recv()

        stats = [l_part[c, g], l_loc[0, g], l_loc[1, g], l_in[0, c, g], l_in[1, c, g]]
        parts = [o_part[c, g], o_loc[0, g], o_loc[1, g], o_in[0, c, g], o_in[1, c, g]]
        peak = functools.reduce(jnp.maximum, stats)
        shares = [jnp.exp2(stat - peak) for stat in stats]
        scale = 1.0 / functools.reduce(jnp.add, shares)
        mixed = functools.reduce(
            jnp.add, [part.astype(jnp.float32) * (share * scale) for part, share in zip(parts, shares)])
        done = mixed.T.astype(jnp.bfloat16)
        for j in range(GROUP):
            staged[:, pl.ds(pl.multiple_of(g * GW + j * HEAD_DIM, HEAD_DIM), HEAD_DIM)] = (
                done[j * rollouts:(j + 1) * rollouts])
        out_copy(g).start()

    loads[0].wait()
    loads[1].wait()
    inner = (c >= 1) & (c + 1 < n)
    outer = jnp.logical_not(inner)
    turn = jnp.where(c == 0, 1, -1)
    arrivals = KV_HEADS * (n - 1)
    ready = WHOLE_AT if n == 4 else KV_HEADS * (n - 2)
    offset = OFFSET if n == 4 else ready + 2 * KV_HEADS
    finals = offset + (FINAL_AT if n == 4 else arrivals + HOP * (n - 1))
    length = max(finals + KV_HEADS, arrivals + HOP * (n - 2) + offset, ready + 2 * KV_HEADS, PASS_AT + 16, NODE_AT + KV_HEADS)
    for load in loads[2:5]:
        load.wait()

    @pl.loop(0, KV_HEADS // 4)
    def _(s):
        for k in range(4):
            vt[4 * s + k] = prefix[1, :, head_cols(4 * s + k)].T
            suffix_item(4 * s + k)

    @pl.loop(0, length)
    def _(u):
        relay(u)
        distance, g = arrival(u, n - 1)
        src = jnp.clip(c + turn * distance, 0, n - 1)
        busy = outer & (u < arrivals)

        @pl.when(busy & (distance == 1))
        def _():
            pair_item(src, g)

        @pl.when(busy & (distance > 1))
        def _():
            single_item(src, g)

        @pl.when(busy)
        def _():
            emit(src, g)

        for j in range(CHUNKS):
            @pl.when(u == PASS_AT + 4 * j)
            def _():
                for k in range(1, chips):
                    peer = lax.rem(b + 2 * k, nb)
                    node_pass(peer, n_pass.at[k], j).wait_recv()
                    node_pass(peer, n_pass.at[k], j).start()

        whole = u - ready

        @pl.when(inner & (whole >= 0) & (whole < 2 * KV_HEADS) & (whole % 2 == 0))
        def _():
            whole_item(whole // 2)

        for side, hops in ((0, n - 1 - c), (1, c)):
            x = u - offset - HOP * hops
            far, h = arrival(x, n - 1)
            dest = n - 1 - far if side == 0 else far
            onward = (dest < c) if side == 0 else (dest > c)

            @pl.when(inner & (x >= 0) & (x < arrivals) & onward)
            def _():
                merge(dest, side, h)

        w = u - jnp.where(inner, NODE_AT, NODE_END)

        @pl.when((w >= 0) & (w < KV_HEADS) & (w % 4 == 0))
        def _():
            for k in range(chips):
                peer = lax.rem(twin + 2 * k, nb)
                for j in range(4 // wide):
                    node_pass(peer, n_pass.at[k], w // wide + j).wait_recv()
            for k in range(4):
                node_item(w + k)

        f = u - finals

        @pl.when((f >= 0) & (f < KV_HEADS))
        def _():
            final(f)

    @pl.loop(0, KV_HEADS)
    def _(g):
        for d in range(1, n):
            @pl.when((c - d >= 0) & (c + 1 < n))
            def _():
                pass_copy(0, c - d, c + 1, g).wait_send()

            @pl.when((c + d < n) & (c >= 1))
            def _():
                pass_copy(1, c + d, c - 1, g).wait_send()

            for copy in result_copies(lax.rem(c + d, n), 0, lax.rem(c + d, n), g):
                copy.wait_send()
        out_copy(g).wait()

    for j in range(CHUNKS):
        for k in range(1, chips):
            node_copy(lax.rem(b + 2 * k, nb), b, n_send.at[k], j).wait_send()
            node_pass(lax.rem(b + 2 * k, nb), n_pass.at[k], j).wait_send()
        node_copy(twin, b, n_send.at[0], j).wait_send()


def on_device(n, nb, prefix_kv, queries, new_kv, suffix_kv, suffix_len, node_kv, node_len, parent, leaf):
    rows = queries.shape[0] * GROUP
    dma = pltpu.SemaphoreType.DMA
    bf16, f32 = jnp.bfloat16, jnp.float32
    return pl.pallas_call(
        functools.partial(kernel, n, nb),
        out_shape=jax.ShapeDtypeStruct(queries.shape, bf16),
        in_specs=[pl.BlockSpec(memory_space=pltpu.HBM)] * 9,
        out_specs=pl.BlockSpec(memory_space=pltpu.HBM),
        scratch_shapes=[
            pltpu.SMEM(suffix_len.shape, jnp.int32),
            pltpu.SMEM(node_len.shape, jnp.int32),
            pltpu.SMEM(parent.shape, jnp.int32),
            pltpu.SMEM(leaf.shape, jnp.int32),
            pltpu.VMEM(new_kv.shape, bf16),
            pltpu.VMEM(prefix_kv.shape, bf16),
            pltpu.VMEM(suffix_kv.shape, bf16),
            pltpu.VMEM((nb,) + node_kv.shape, bf16),
            pltpu.VMEM((KV_HEADS, HEAD_DIM, prefix_kv.shape[1]), bf16),
            pltpu.VMEM((n,) + queries.shape, bf16),
            pltpu.VMEM((n, KV_HEADS, HEAD_DIM, rows), f32),
            pltpu.VMEM((n, KV_HEADS, 1, rows), f32),
            pltpu.VMEM((n, KV_HEADS, HEAD_DIM, rows), bf16),
            pltpu.VMEM((n, KV_HEADS, 1, rows), f32),
            pltpu.VMEM((2, n, KV_HEADS, HEAD_DIM, rows), bf16),
            pltpu.VMEM((2, n, KV_HEADS, 1, rows), f32),
            pltpu.VMEM((2, KV_HEADS, HEAD_DIM, rows), f32),
            pltpu.VMEM((2, KV_HEADS, 1, rows), f32),
            pltpu.VMEM(queries.shape, bf16),
            dma((9,)),
            dma((KV_HEADS,)),
            dma((2, n, KV_HEADS)),
            dma((n, KV_HEADS)),
            dma((n, KV_HEADS)),
            dma((2, n, KV_HEADS)),
            dma((n, KV_HEADS)),
            dma((2, n, KV_HEADS)),
            dma((nb // 2, CHUNKS)),
            dma((nb // 2, CHUNKS)),
            dma((nb, CHUNKS)),
        ],
        compiler_params=pltpu.CompilerParams(
            collective_id=0, has_side_effects=True, vmem_limit_bytes=63 * 1024 * 1024),
    )(suffix_len, node_len, parent, leaf, queries, new_kv, prefix_kv, suffix_kv, node_kv)


def solution(mesh):
    return jax.shard_map(
        functools.partial(on_device, mesh.shape["ctx"], mesh.shape["branch"]),
        mesh=mesh,
        in_specs=(
            P(None, ("parts", "ctx"), None),
            P(("parts", "ctx", "branch"), None),
            P(None, ("parts", "ctx", "branch"), None),
            P(None, ("parts", "ctx", "branch"), None, None),
            P(("parts", "ctx", "branch")),
            P(None, ("parts", "branch"), None, None),
            P("parts"),
            P("parts"),
            P(("parts", "ctx", "branch")),
        ),
        out_specs=P(("parts", "ctx", "branch"), None),
        check_vma=False,
    )
```
